512 devices in a mesh: section: 2 (over x_lo), expert: 64 (over z, x_hi, core), dp: 4 (over y).
Axes of the slice: x: 4 (x_hi: 2, x_lo: 2; x = x_hi * 2 + x_lo), y: 4, z: 16, core: 2. Of those that a mesh axis runs over, the one named last changes fastest.
Arguments:
- tokens: bfloat16 [2, 32768, 3584], P('section', ('expert', 'dp')), may hold values from -6 to 6
- grad_out: bfloat16 [2, 32768, 3584], P('section', ('expert', 'dp')), may hold values from -6 to 6
- expert_ids: int32 [2, 32768, 2], P('section', ('expert', 'dp')), may hold values from 0 to 31, all different within a row; in each aligned block of 128 rows (0 to 127, 128 to 255, ..., all dimensions but the last counted through in order) at most 9 rows name the same one
- gate_values: float32 [2, 32768, 2], P('section', ('expert', 'dp')), may hold values from 0.1 to 1
- w_in: bfloat16 [2, 64, 1792, 1024], P('section', 'expert', None, 'dp'), may hold values from -0.09375 to 0.09375
- w_out_t: bfloat16 [2, 64, 1792, 1024], P('section', 'expert', None, 'dp'), may hold values from -0.1875 to 0.1875
Outputs:
- handed_grad: bfloat16 [2, 32768, 3584], P('section', ('expert', 'dp'))
The draws below stay inside these ranges and needn't reach their ends.
Inputs may be any that keep to these rules, and one draw needn't show every extreme that they name: `expert_ids`: each token names 2 different experts; in each aligned block of 128 tokens (the tokens of one device) no expert is named more than 9 times, a bound that some block reaches.
All inputs are finite; a program needn't handle non-finite values.
Results may differ from the reference program's by a relative error of at most 0.0051.
Values may be sent and summed in bfloat16 or wider, within the bound.
A program may use at most 128 MiB of HBM per device.

```python
import math
import jax
import jax.numpy as jnp
import numpy as np
from jax import lax

D = 3584
FF = 1024
TOP = 2
TOK_DEV = 128
EXPERTS = 32
CAP = 9
TOKENS = 32768
N_SECTION = 2


def block_scale(own_key, dims, cuts, least, top_value):
    def one(dim, blocks):
        steps = jax.random.uniform(jax.random.fold_in(jax.random.fold_in(own_key, 6), dim), (blocks,), jnp.float32, least / len(cuts), top_value / len(cuts))
        return jnp.repeat(jnp.exp(steps), dims[dim] // blocks).reshape((-1,) + (1,) * (len(dims) - dim - 1))

    loudness = one(*cuts[0])
    for cut in cuts[1:]:
        loudness = loudness * one(*cut)
    return loudness


def deal_out(key, own, number, rows, number_of, top, limit, slope):
    ranking = jax.random.permutation(key, number_of)
    heavy_load, common = shares(number_of, rows * top, limit, slope, True), shares(number_of, rows * top, limit, slope, False)
    places = jnp.arange(number_of)

    def named(tallies, turn):
        used = int((tallies > 0).sum())
        fixed = max(1, used // 4)
        passed = fixed + (places - fixed + turn * (used - fixed)) % max(1, number_of - fixed)
        return jnp.zeros((number_of,), jnp.int32).at[ranking[jnp.where(places < fixed, places, passed)]].set(jnp.asarray(tallies, jnp.int32))

    tallies = jnp.where(number % 4 == 0, named(heavy_load, number // 4), named(common, number - number // 4 - 1))
    mixed = jax.random.permutation(jax.random.fold_in(own, 3), number_of)
    source_of, sink = mixed[0:number_of // 2 * 2:2], mixed[1:number_of // 2 * 2:2]
    room = jnp.minimum(tallies[source_of] - 1, limit - tallies[sink]) // 2
    room = jnp.where((source_of == ranking[0]) | (sink == ranking[0]) | (tallies[sink] == 0), 0, jnp.maximum(room, 0))
    passed = jax.random.randint(jax.random.fold_in(own, 4), (number_of // 2,), 0, 1 << 20) % (room + 1)
    tallies = tallies.at[source_of].add(-passed).at[sink].add(passed)
    members = jnp.searchsorted(jnp.cumsum(tallies), jnp.arange(rows * top), side="right").astype(jnp.int32)
    grid = members.reshape(top, rows).T
    grid = grid[jax.random.permutation(jax.random.fold_in(own, 1), rows)]
    turn = jax.random.randint(jax.random.fold_in(own, 2), (rows, 1), 0, top)
    return jnp.take_along_axis(grid, (jnp.arange(top)[None, :] + turn) % top, axis=1)


def shares(number_of, total, most, skew, full):
    weights = [(1 << 20) // math.isqrt(grade ** skew) + 1 for grade in range(1, number_of + 1)]
    largest = most if full else min(most, max(-(-total // number_of), total * weights[0] // sum(weights)))
    least = 1 if total - largest >= number_of - 1 else 0
    counts, spare = [largest] + [least] * (number_of - 1), total - largest - least * (number_of - 1)
    while spare > 0:
        candidates = [i for i in range(1, number_of) if counts[i] < largest] or [i for i in range(1, number_of) if counts[i] < most]
        whole, left = sum([weights[i] for i in candidates]), spare
        for i in candidates:
            addition = min(most - counts[i], max(1, left * weights[i] // whole), spare)
            counts[i] = counts[i] + addition
            spare = spare - addition
    return np.array(counts)


def gaussian(own_key, extent, deviation, most, shards=(), kind=jnp.bfloat16):
    drawn = jax.random.normal(own_key, extent, jnp.float32) * deviation
    if len(shards) > 0:
        drawn = block_scale(own_key, extent, shards, -0.22, 0.18) * drawn
    return jnp.clip(drawn, min=-most, max=most).astype(kind)


def setup_inputs(seed: int = 0) -> dict:
    splits = jax.random.split(jax.random.key(seed), 7)
    tokens = gaussian(splits[0], (N_SECTION, TOKENS, D), 1.0, 6.0, ((0, 2), (1, 256)))
    grad_out = gaussian(splits[1], (N_SECTION, TOKENS, D), 1.0, 6.0, ((0, 2), (1, 256)))
    expert_ids_keys = jax.random.split(jax.random.fold_in(splits[2], 1), N_SECTION * TOKENS // TOK_DEV)
    expert_ids_turns = jax.random.permutation(jax.random.fold_in(splits[2], 3), N_SECTION * TOKENS // TOK_DEV)
    expert_ids = jax.vmap(lambda own, number: deal_out(jax.random.fold_in(splits[2], 2), own, number, TOK_DEV, EXPERTS, TOP, CAP, 1))(expert_ids_keys, expert_ids_turns).reshape((N_SECTION, TOKENS, TOP))
    gate_values = jnp.clip(0.1 + 0.9 * jax.random.uniform(splits[3], (N_SECTION, TOKENS, TOP), jnp.float32) ** block_scale(splits[3], (N_SECTION, TOKENS, TOP), ((0, 2), (1, 256)), -0.2, 0.2), 0.1, 1.0)
    w_in = gaussian(splits[4], (N_SECTION, 2 * EXPERTS, D // 2, FF), D ** -0.5, 0.09375, ((0, 2), (1, 64), (3, 4)))
    w_out_t = gaussian(splits[5], (N_SECTION, 2 * EXPERTS, D // 2, FF), FF ** -0.5, 0.1875, ((0, 2), (1, 64), (3, 4)))
    return {"tokens": tokens, "grad_out": grad_out, "expert_ids": expert_ids, "gate_values": gate_values, "w_in": w_in, "w_out_t": w_out_t}


def rounded(value):
    return lax.optimization_barrier(value.astype(jnp.bfloat16)).astype(jnp.float32)

def silu_slope(pre):
    sig = jax.nn.sigmoid(pre)
    return sig * (1.0 + pre * (1.0 - sig))

def section_grad(tokens, grad_out, expert_ids, gate_values, w_in, w_out_t):
    flat_ids = expert_ids.reshape(-1).astype(jnp.int32)
    total_rows = flat_ids.shape[0]
    per_block = TOK_DEV * TOP
    blocks = total_rows // per_block
    onehot = (flat_ids[:, None] == jnp.arange(EXPERTS, dtype=jnp.int32)[None, :]).astype(jnp.int32)
    onehot = onehot.reshape(blocks, per_block, EXPERTS)
    before = jnp.cumsum(onehot, axis=1) - onehot
    rank = lax.optimization_barrier(jnp.sum(before * onehot, axis=2)).reshape(-1).astype(jnp.int32)
    block_of = jnp.arange(total_rows, dtype=jnp.int32) // per_block
    table = jnp.full((EXPERTS, blocks * CAP), -1, jnp.int32)
    table = table.at[flat_ids, block_of * CAP + rank].set(jnp.arange(total_rows, dtype=jnp.int32))
    half = D // 2
    w_pairs = w_in.reshape(EXPERTS, D, FF)
    v_pairs = w_out_t.reshape(EXPERTS, D, FF)
    grad32 = grad_out.astype(jnp.float32)
    gate_flat = gate_values.reshape(-1)

    def one_expert(total, inputs):
        slots, w_one, v_one = inputs
        valid = slots >= 0
        row_index = jnp.where(valid, slots, 0).astype(jnp.int32)
        token_index = (row_index // TOP).astype(jnp.int32)
        gate = jnp.where(valid, gate_flat[row_index], 0.0)
        x_rows = tokens[token_index].astype(jnp.float32)
        g_rows = rounded(gate[:, None] * grad32[token_index])
        w32 = w_one.astype(jnp.float32)
        v32 = v_one.astype(jnp.float32)
        pre = rounded(x_rows[:, :half] @ w32[:half]) + rounded(x_rows[:, half:] @ w32[half:])
        hid = rounded(g_rows[:, :half] @ v32[:half]) + rounded(g_rows[:, half:] @ v32[half:])
        act = rounded(hid * silu_slope(pre))
        back = rounded(act @ w32.T) * valid[:, None].astype(jnp.float32)
        return (total.at[token_index].add(back), None)
    start = jnp.zeros(tokens.shape, jnp.float32)
    total, _ = lax.scan(one_expert, start, (table, w_pairs, v_pairs))
    return (grad32 + total).astype(jnp.bfloat16)

def reference(tokens, grad_out, expert_ids, gate_values, w_in, w_out_t):
    first = section_grad(tokens[0], grad_out[0], expert_ids[0], gate_values[0], w_in[0], w_out_t[0])
    second = section_grad(tokens[1], grad_out[1], expert_ids[1], gate_values[1], w_in[1], w_out_t[1])
    return jnp.stack([second, first])
```

```python
import functools

import jax
import jax.numpy as jnp
from jax import lax
from jax.experimental import pallas as pl
from jax.experimental.pallas import tpu as pltpu
from jax.sharding import PartitionSpec as P

MESH = pl.DeviceIdType.MESH
F32 = jnp.float32
BF16 = jnp.bfloat16
GROUP = 8


def silu_slope(pre):
    sig = 1.0 / (1.0 + jnp.exp(-pre))
    return sig * (1.0 + pre * (1.0 - sig))


def kernel(
    ring,
    n_dp,
    tok_ref,
    grad_ref,
    ids_ref,
    gate_ref,
    win_ref,
    wout_ref,
    out_ref,
    xg,
    partner_grad,
    combine,
    partner_combine,
    send_a,
    send_b,
    recv_a,
    recv_b,
    back_a,
    back_b,
    home_a,
    home_b,
    w_full,
    v_full,
    act,
    row_scr,
    home_scr,
    load_sem,
    send_a_sem,
    send_b_sem,
    recv_a_sem,
    recv_b_sem,
    back_a_sem,
    back_b_sem,
    home_a_sem,
    home_b_sem,
    hand_send_sem,
    hand_recv_sem,
    wdp_send_sem,
    wdp_recv_sem,
    wcore_send_sem,
    wcore_recv_sem,
):
    n_tok, width = tok_ref.shape
    half = width // 2
    quarter = win_ref.shape[1]
    chips = 2 * ring
    chunks = chips // GROUP
    section = lax.axis_index("section")
    me = lax.axis_index("expert")
    dp = lax.axis_index("dp")
    core = lax.rem(me, 2)
    my_chip = me // 2
    my_xh = lax.rem(my_chip, 2)
    my_z = my_chip // 2
    other_section = 1 - section
    other_core = me + 1 - 2 * core

    barrier = pltpu.get_barrier_semaphore()

    @pl.loop(0, chips)
    def _(chip):
        @pl.when(chip != my_chip)
        def _():
            pl.semaphore_signal(
                barrier, inc=1, device_id={"expert": 2 * chip + core}, device_id_type=MESH
            )

        pl.semaphore_signal(
            barrier,
            inc=1,
            device_id={"section": other_section, "expert": 2 * chip + core},
            device_id_type=MESH,
        )

    for step in range(1, n_dp):
        pl.semaphore_signal(
            barrier, inc=1, device_id={"dp": lax.rem(dp + step, n_dp)}, device_id_type=MESH
        )
    pl.semaphore_signal(barrier, inc=1, device_id={"expert": other_core}, device_id_type=MESH)

    load_tok = pltpu.make_async_copy(tok_ref, xg.at[pl.ds(0, n_tok)], load_sem.at[0])
    load_grad = pltpu.make_async_copy(grad_ref, xg.at[pl.ds(n_tok, n_tok)], load_sem.at[1])
    load_win = pltpu.make_async_copy(win_ref, w_full.at[dp, core], load_sem.at[2])
    load_wout = pltpu.make_async_copy(wout_ref, v_full.at[dp, core], load_sem.at[3])
    load_tok.start()
    load_grad.start()
    load_win.start()
    load_wout.start()

    ids = jnp.concatenate([ids_ref[0:1, :], ids_ref[1:2, :]], axis=1)
    flat = 2 * n_tok
    hot = (lax.broadcasted_iota(jnp.int32, (chips, flat), 0) == ids).astype(F32)
    earlier = (
        lax.broadcasted_iota(jnp.int32, (flat, flat), 0)
        < lax.broadcasted_iota(jnp.int32, (flat, flat), 1)
    ).astype(F32)
    before = jnp.dot(hot.astype(BF16), earlier.astype(BF16), preferred_element_type=F32)
    rank = jnp.sum(hot * before, axis=0, keepdims=True).astype(jnp.int32)
    apart = (ids // 2 - my_z + ring) % ring
    hops = jnp.minimum(apart, ring - apart)
    place = 2 * (ring // 2 - hops) - (apart < ring // 2).astype(jnp.int32)
    unit = 2 * place + ids % 2
    extra = rank >= GROUP
    full_rows = chips * 2 * GROUP
    row_x = jnp.where(extra, full_rows + 2 * unit, unit * 2 * GROUP + rank)
    row_g = jnp.where(extra, row_x + 1, row_x + GROUP)
    slot = jnp.where(extra, chips * GROUP + ids, ids * GROUP + rank)

    slot_rows = combine.shape[1]
    slot_iota = lax.broadcasted_iota(jnp.int32, (slot_rows, n_tok), 0)
    picks = (slot_iota == slot[:, :n_tok]).astype(F32) + (slot_iota == slot[:, n_tok:]).astype(F32)
    combine[...] = jnp.transpose(picks).astype(BF16)

    pl.semaphore_wait(barrier, 2 * chips - 1 + n_dp)

    def weight_send(mat, y_from, target, to_core):
        full = (w_full, v_full)[mat]
        if to_core:
            return pltpu.make_async_remote_copy(
                src_ref=full.at[y_from, core],
                dst_ref=full.at[y_from, core],
                send_sem=wcore_send_sem.at[mat, y_from],
                recv_sem=wcore_recv_sem.at[mat, y_from],
                device_id={"expert": other_core},
                device_id_type=MESH,
            )
        return pltpu.make_async_remote_copy(
            src_ref=(win_ref, wout_ref)[mat],
            dst_ref=full.at[dp, core],
            send_sem=wdp_send_sem.at[mat, target],
            recv_sem=wdp_recv_sem.at[mat, dp],
            device_id={"dp": target},
            device_id_type=MESH,
        )

    steps = [s for pair in zip(range(1, n_dp), range(n_dp - 1, 0, -1)) for s in pair]
    steps = list(dict.fromkeys(steps))
    for step in steps:
        for mat in range(2):
            weight_send(mat, None, lax.rem(dp + step, n_dp), False).start()

    def hand(which):
        return pltpu.make_async_remote_copy(
            src_ref=(grad_ref, combine)[which],
            dst_ref=(partner_grad, partner_combine)[which],
            send_sem=hand_send_sem.at[which],
            recv_sem=hand_recv_sem.at[which],
            device_id={"section": other_section},
            device_id_type=MESH,
        )

    hand(0).start()
    hand(1).start()

    load_tok.wait()
    load_grad.wait()

    def shift_of(place):
        odd = place % 2
        hop = ring // 2 - (place + odd) // 2
        return jnp.where(odd == 1, hop, ring - hop) % ring

    def mirror_of(place):
        odd = place % 2
        inner = jnp.where(odd == 1, place + 1, place - 1)
        return jnp.where((place == 0) | (place == ring - 1), place, inner)

    def dispatch(unit, own):
        place = unit // 2
        xh = unit % 2
        chip = 2 * ((my_z + shift_of(place)) % ring) + xh
        there = 2 * mirror_of(place) + my_xh
        pair_a = (send_a.at[unit], recv_a.at[there // GROUP, there % GROUP])
        pair_b = (send_b.at[unit], recv_b.at[there])
        pairs = (
            (pair_a, (send_a_sem, recv_a_sem)),
            (pair_b, (send_b_sem, recv_b_sem)),
        )
        if own:
            return [
                pltpu.make_async_copy(*pair, sems[1].at[there]) for pair, sems in pairs
            ]
        return [
            pltpu.make_async_remote_copy(
                src_ref=pair[0],
                dst_ref=pair[1],
                send_sem=sems[0].at[unit],
                recv_sem=sems[1].at[there],
                device_id={"expert": 2 * chip + core},
                device_id_type=MESH,
            )
            for pair, sems in pairs
        ]

    own_unit = 2 * (ring - 1) + my_xh
    rows = GROUP * 2 * GROUP
    block = 512 if width % 512 == 0 else 256

    @pl.loop(0, chunks)
    def _(chunk):
        local_row = lax.broadcasted_iota(jnp.int32, (rows + 2 * GROUP, 1), 0)
        spare = local_row >= rows
        row_id = jnp.where(
            spare, full_rows + chunk * 2 * GROUP + local_row - rows, chunk * rows + local_row
        )
        is_x = jnp.where(spare, local_row % 2, local_row % (2 * GROUP) // GROUP) == 0
        x0 = row_id == row_x[:, :n_tok]
        x1 = row_id == row_x[:, n_tok:]
        g0 = row_id == row_g[:, :n_tok]
        g1 = row_id == row_g[:, n_tok:]
        pick = jnp.concatenate(
            [x0.astype(F32) + x1.astype(F32), g0.astype(F32) + g1.astype(F32)], axis=1
        ).astype(BF16)
        gate = jnp.where(g0, gate_ref[0:1, :], 0.0) + jnp.where(g1, gate_ref[1:2, :], 0.0)
        gate = jnp.sum(gate, axis=1, keepdims=True)
        scale = jnp.where(is_x, 1.0, gate)
        for lane in range(0, width, block):
            part = jnp.dot(pick, xg[:, lane : lane + block], preferred_element_type=F32) * scale
            send_a[pl.ds(chunk * GROUP, GROUP), :, lane : lane + block] = (
                part[:rows].astype(BF16).reshape(GROUP, 2 * GROUP, block)
            )
            row_scr[:, lane : lane + block] = part[rows:]
        for i in range(GROUP):
            send_b[chunk * GROUP + i] = row_scr[2 * i : 2 * i + 2, :].astype(BF16)

        @pl.loop(0, GROUP)
        def _(i):
            unit = chunk * GROUP + i
            own = unit == own_unit

            @pl.when(own)
            def _():
                for copy in dispatch(unit, True):
                    copy.start()

            @pl.when(jnp.logical_not(own))
            def _():
                for copy in dispatch(unit, False):
                    copy.start()

    load_win.wait()
    load_wout.wait()
    for mat in range(2):
        weight_send(mat, dp, None, True).start()
    for step in steps:
        y_from = lax.rem(dp + n_dp - step, n_dp)
        for mat in range(2):
            pltpu.make_async_remote_copy(
                src_ref=(win_ref, wout_ref)[mat],
                dst_ref=(w_full, v_full)[mat].at[y_from, core],
                send_sem=wdp_send_sem.at[mat, y_from],
                recv_sem=wdp_recv_sem.at[mat, y_from],
                device_id={"dp": y_from},
                device_id_type=MESH,
            ).wait_recv()
            weight_send(mat, y_from, None, True).start()
    for y_from in range(n_dp):
        for mat in range(2):
            full = (w_full, v_full)[mat]
            pltpu.make_async_remote_copy(
                src_ref=full.at[y_from, 1 - core],
                dst_ref=full.at[y_from, 1 - core],
                send_sem=wcore_send_sem.at[mat, y_from],
                recv_sem=wcore_recv_sem.at[mat, y_from],
                device_id={"expert": other_core},
                device_id_type=MESH,
            ).wait_recv()

    def give_back(unit):
        chip = 2 * ((my_z + shift_of(unit // 2)) % ring) + unit % 2
        return [
            pltpu.make_async_remote_copy(
                src_ref=source.at[unit],
                dst_ref=home.at[my_chip],
                send_sem=sems[0].at[unit],
                recv_sem=sems[1].at[my_chip],
                device_id={"section": other_section, "expert": 2 * chip + core},
                device_id_type=MESH,
            )
            for source, home, sems in (
                (back_a, home_a, (back_a_sem, home_a_sem)),
                (back_b, home_b, (back_b_sem, home_b_sem)),
            )
        ]

    tall = 2 * GROUP * (GROUP + 1)
    short = GROUP * (GROUP + 1)

    @pl.loop(0, chunks)
    def _(chunk):
        @pl.loop(0, GROUP)
        def _(i):
            unit = chunk * GROUP + i
            a_ref = recv_a.at[chunk, i]
            pltpu.make_async_copy(a_ref, a_ref, recv_a_sem.at[unit]).wait()
            b_ref = recv_b.at[unit]
            pltpu.make_async_copy(b_ref, b_ref, recv_b_sem.at[unit]).wait()

        for i in range(GROUP):
            pair = recv_b[chunk * GROUP + i].astype(F32)
            row_scr[i : i + 1, :] = pair[0:1]
            row_scr[GROUP + i : GROUP + i + 1, :] = pair[1:2]
        recv_a[chunk, GROUP] = row_scr[...].astype(BF16)

        @pl.loop(0, n_dp)
        def _(y):
            def product(full, first):
                total = None
                for h in range(2):
                    left = recv_a[chunk, :, :, h * half : (h + 1) * half].reshape(tall, half)
                    part = jnp.dot(left, full[y, h], preferred_element_type=F32)
                    part = part.reshape(GROUP + 1, 2 * GROUP, quarter)
                    part = part[:, first : first + GROUP, :].astype(BF16).astype(F32)
                    total = part if total is None else total + part
                return total

            pre = product(w_full, 0)
            hid = product(v_full, GROUP)
            act[y] = (hid * silu_slope(pre)).reshape(short, quarter).astype(BF16)

        lanes = 256 if half % 256 == 0 else half
        for h in range(2):
            for lane in range(0, half, lanes):
                total = None
                for y in range(n_dp):
                    part = lax.dot_general(
                        act[y],
                        w_full[y, h, lane : lane + lanes, :],
                        (((1,), (1,)), ((), ())),
                        preferred_element_type=F32,
                    )
                    total = part if total is None else total + part
                left = h * half + lane
                back_a[pl.ds(chunk * GROUP, GROUP), :, left : left + lanes] = (
                    total[: GROUP * GROUP].reshape(GROUP, GROUP, lanes).astype(BF16)
                )
                row_scr[:GROUP, left : left + lanes] = total[GROUP * GROUP :]
        for i in range(GROUP):
            back_b[chunk * GROUP + i] = jnp.concatenate(
                [row_scr[i : i + 1, :half], row_scr[i : i + 1, half:]], axis=0
            ).astype(BF16)

        @pl.loop(0, GROUP)
        def _(i):
            for copy in give_back(chunk * GROUP + i):
                copy.start()

    hand(0).wait_recv()
    hand(1).wait_recv()

    @pl.loop(0, chips)
    def _(chip):
        a_ref = home_a.at[chip]
        pltpu.make_async_copy(a_ref, a_ref, home_a_sem.at[chip]).wait()
        b_ref = home_b.at[chip]
        pltpu.make_async_copy(b_ref, b_ref, home_b_sem.at[chip]).wait()

    for chip in range(chips):
        pair = home_b[chip].astype(F32)
        home_scr[chip : chip + 1, :half] = pair[0:1]
        home_scr[chip : chip + 1, half:] = pair[1:2]
    for lane in range(0, width, block):
        span = slice(lane, lane + block)
        main = home_a[:, :, span].astype(F32).reshape(chips * GROUP, block).astype(BF16)
        total = jnp.dot(
            partner_combine[:, : chips * GROUP], main, preferred_element_type=F32
        ) + jnp.dot(
            partner_combine[:, chips * GROUP : chips * GROUP + chips],
            home_scr[:, span].astype(BF16),
            preferred_element_type=F32,
        )
        out_ref[:, span] = (partner_grad[:, span].astype(F32) + total).astype(BF16)

    hand(0).wait_send()
    hand(1).wait_send()
    for step in range(1, n_dp):
        for mat in range(2):
            weight_send(mat, None, lax.rem(dp + step, n_dp), False).wait_send()
    for y_from in range(n_dp):
        for mat in range(2):
            weight_send(mat, y_from, None, True).wait_send()

    @pl.loop(0, chips)
    def _(unit):
        @pl.when(unit != own_unit)
        def _():
            for copy in dispatch(unit, False):
                copy.wait_send()

        for copy in give_back(unit):
            copy.wait_send()


def call(ring, n_dp, tokens, grads, ids, gates, w_in, w_out):
    n_tok, width = tokens.shape
    half = width // 2
    quarter = w_in.shape[1]
    chips = 2 * ring
    chunks = chips // GROUP
    slot_rows = -(-(chips * (GROUP + 1)) // 128) * 128
    dma = pltpu.SemaphoreType.DMA
    any_spec = pl.BlockSpec(memory_space=pl.ANY)
    vmem_spec = pl.BlockSpec(memory_space=pltpu.VMEM)
    return pl.pallas_call(
        functools.partial(kernel, ring, n_dp),
        out_shape=jax.ShapeDtypeStruct((n_tok, width), BF16),
        in_specs=[any_spec, any_spec, vmem_spec, vmem_spec, any_spec, any_spec],
        out_specs=vmem_spec,
        scratch_shapes=[
            pltpu.VMEM((2 * n_tok, width), BF16),
            pltpu.VMEM((n_tok, width), BF16),
            pltpu.VMEM((n_tok, slot_rows), BF16),
            pltpu.VMEM((n_tok, slot_rows), BF16),
            pltpu.VMEM((chips, 2 * GROUP, width), BF16),
            pltpu.VMEM((chips, 2, width), BF16),
            pltpu.VMEM((chunks, GROUP + 1, 2 * GROUP, width), BF16),
            pltpu.VMEM((chips, 2, width), BF16),
            pltpu.VMEM((chips, GROUP, width), BF16),
            pltpu.VMEM((chips, 2, half), BF16),
            pltpu.VMEM((chips, GROUP, width), BF16),
            pltpu.VMEM((chips, 2, half), BF16),
            pltpu.VMEM((n_dp, 2, half, quarter), BF16),
            pltpu.VMEM((n_dp, 2, half, quarter), BF16),
            pltpu.VMEM((n_dp, GROUP * (GROUP + 1), quarter), BF16),
            pltpu.VMEM((2 * GROUP, width), F32),
            pltpu.VMEM((chips, width), F32),
            dma((4,)),
            dma((chips,)),
            dma((chips,)),
            dma((chips,)),
            dma((chips,)),
            dma((chips,)),
            dma((chips,)),
            dma((chips,)),
            dma((chips,)),
            dma((2,)),
            dma((2,)),
            dma((2, n_dp)),
            dma((2, n_dp)),
            dma((2, n_dp)),
            dma((2, n_dp)),
        ],
        compiler_params=pltpu.CompilerParams(
            collective_id=0, has_side_effects=True, vmem_limit_bytes=56 * 1024 * 1024
        ),
        name="routed_backward",
    )(tokens, grads, ids, gates, w_in, w_out)


def solution(mesh):
    ring = mesh.shape["expert"] // 4
    n_dp = mesh.shape["dp"]

    def body(tokens, grad_out, expert_ids, gate_values, w_in, w_out_t):
        handed = call(
            ring,
            n_dp,
            tokens[0],
            grad_out[0],
            expert_ids[0].T,
            gate_values[0].T,
            w_in[0, 0],
            w_out_t[0, 0],
        )
        return handed[None]

    return jax.shard_map(
        body,
        mesh=mesh,
        in_specs=(
            P("section", ("expert", "dp"), None),
            P("section", ("expert", "dp"), None),
            P("section", ("expert", "dp"), None),
            P("section", ("expert", "dp"), None),
            P("section", "expert", None, "dp"),
            P("section", "expert", None, "dp"),
        ),
        out_specs=P("section", ("expert", "dp"), None),
        check_vma=False,
    )
```

```python
import functools

import jax
import jax.numpy as jnp
from jax import lax
from jax.experimental import pallas as pl
from jax.experimental.pallas import tpu as pltpu
from jax.sharding import PartitionSpec as P

MESH = pl.DeviceIdType.MESH
F32 = jnp.float32
BF16 = jnp.bfloat16
GROUP = 8
REACH = 2


def silu_slope(pre):
    sig = 1.0 / (1.0 + jnp.exp(-pre))
    return sig * (1.0 + pre * (1.0 - sig))


def kernel(
    ring,
    n_dp,
    tok_ref,
    grad_ref,
    ids_ref,
    gate_ref,
    win_ref,
    wout_ref,
    out_ref,
    xg,
    partner_grad,
    combine,
    partner_combine,
    send_a,
    send_b,
    recv_a,
    recv_b,
    back_a,
    back_b,
    home_a,
    home_b,
    w_full,
    v_full,
    act,
    row_scr,
    home_scr,
    load_sem,
    send_a_sem,
    send_b_sem,
    recv_a_sem,
    recv_b_sem,
    back_a_sem,
    back_b_sem,
    home_a_sem,
    home_b_sem,
    hand_send_sem,
    hand_recv_sem,
    wz_send_sem,
    wz_recv_sem,
    wy_send_sem,
    wy_recv_sem,
):
    n_tok, width = tok_ref.shape
    half = width // 2
    quarter = win_ref.shape[1]
    chips = 2 * ring
    far = ring // 2
    chunks = chips // GROUP
    section = lax.axis_index("section")
    me = lax.axis_index("expert")
    dp = lax.axis_index("dp")
    core = me % 2
    my_xh = me // 2 % 2
    my_z = me // 4
    other_section = 1 - section
    dp_up, dp_down = (dp + 1) % n_dp, (dp + n_dp - 1) % n_dp

    side = 1 - 2 * core
    host_z = (my_z + REACH * side + ring) % ring
    host_chip = 2 * host_z + my_xh

    def index_of(z, xh, which_core):
        return 4 * ((z + 2 * ring) % ring) + 2 * xh + which_core

    def steps_of(place):
        odd = place % 2
        hop = far - (place + odd) // 2
        return jnp.where((odd == 1) | (place == 0), hop, -hop)

    def target_of(unit):
        d = steps_of(unit // 2)
        to_side = jnp.where(
            d == far, core, jnp.where(d == 0, 1 - core, (d < 0).astype(jnp.int32))
        )
        expert = index_of(my_z + d - REACH * (1 - 2 * to_side), unit % 2, to_side)
        even = (d == far) | (d == 0)
        spot = jnp.where(
            even,
            jnp.where(d == 0, 2, 0) + my_xh,
            4 * (far - jnp.abs(d)) + 2 * core + my_xh,
        )
        return expert, spot

    def source_of(spot):
        step = spot // 4
        d = jnp.where(step == 0, jnp.where(spot < 2, far, 0), side * (far - step))
        their_core = jnp.where(
            step == 0, jnp.where(spot < 2, core, 1 - core), spot // 2 % 2
        )
        return index_of(host_z - d, spot % 2, their_core)

    barrier = pltpu.get_barrier_semaphore()

    def greet(**where):
        pl.semaphore_signal(barrier, inc=1, device_id=where, device_id_type=MESH)

    for where in (0, 1):
        greet(expert=index_of(host_z, my_xh, where))
    for where in (dp_up, dp_down):
        greet(dp=where)
    greet(section=other_section)

    @pl.loop(0, chips)
    def _(i):
        expert = source_of(i)

        @pl.when(expert != me)
        def _():
            greet(expert=expert)

        greet(section=other_section, expert=target_of(i)[0])

    load_tok = pltpu.make_async_copy(tok_ref, xg.at[pl.ds(0, n_tok)], load_sem.at[0])
    load_grad = pltpu.make_async_copy(grad_ref, xg.at[pl.ds(n_tok, n_tok)], load_sem.at[1])
    load_tok.start()
    load_grad.start()

    ids = jnp.concatenate([ids_ref[0:1, :], ids_ref[1:2, :]], axis=1)
    flat = 2 * n_tok
    hot = (lax.broadcasted_iota(jnp.int32, (chips, flat), 0) == ids).astype(F32)
    earlier = (
        lax.broadcasted_iota(jnp.int32, (flat, flat), 0)
        < lax.broadcasted_iota(jnp.int32, (flat, flat), 1)
    ).astype(F32)
    before = jnp.dot(hot.astype(BF16), earlier.astype(BF16), preferred_element_type=F32)
    rank = jnp.sum(hot * before, axis=0, keepdims=True).astype(jnp.int32)
    apart = (ids // 2 - my_z + ring) % ring
    hops = jnp.minimum(apart, ring - apart)
    place = 2 * (far - hops) - (apart < far).astype(jnp.int32)
    unit = 2 * place + ids % 2
    extra = rank >= GROUP
    full_rows = chips * 2 * GROUP
    row_x = jnp.where(extra, full_rows + 2 * unit, unit * 2 * GROUP + rank)
    row_g = jnp.where(extra, row_x + 1, row_x + GROUP)
    slot = jnp.where(extra, chips * GROUP + ids, ids * GROUP + rank)

    slot_rows = combine.shape[1]
    slot_iota = lax.broadcasted_iota(jnp.int32, (slot_rows, n_tok), 0)
    picks = (slot_iota == slot[:, :n_tok]).astype(F32) + (slot_iota == slot[:, n_tok:]).astype(F32)
    combine[...] = jnp.transpose(picks).astype(BF16)

    pl.semaphore_wait(barrier, 2 * chips - 1 + 5)

    def weight_send(mat, to_side):
        return pltpu.make_async_remote_copy(
            src_ref=(win_ref, wout_ref)[mat],
            dst_ref=(w_full, v_full)[mat].at[dp, core],
            send_sem=wz_send_sem.at[mat, to_side],
            recv_sem=wz_recv_sem.at[mat, core],
            device_id={
                "expert": index_of(my_z - REACH * (1 - 2 * to_side), my_xh, to_side)
            },
            device_id_type=MESH,
        )

    def weight_pass(mat, h, of_dp, up):
        part = (w_full, v_full)[mat].at[of_dp, h]
        return pltpu.make_async_remote_copy(
            src_ref=part,
            dst_ref=part,
            send_sem=wy_send_sem.at[mat, h, of_dp, up],
            recv_sem=wy_recv_sem.at[mat, h, of_dp],
            device_id={"dp": dp_up if up else dp_down},
            device_id_type=MESH,
        )

    for mat in range(2):
        for to_side in range(2):
            weight_send(mat, to_side).start()

    def hand(which):
        return pltpu.make_async_remote_copy(
            src_ref=(grad_ref, combine)[which],
            dst_ref=(partner_grad, partner_combine)[which],
            send_sem=hand_send_sem.at[which],
            recv_sem=hand_recv_sem.at[which],
            device_id={"section": other_section},
            device_id_type=MESH,
        )

    hand(0).start()
    hand(1).start()

    load_tok.wait()
    load_grad.wait()

    def dispatch(unit, own):
        expert, spot = target_of(unit)
        pairs = (
            (send_a.at[unit], recv_a.at[spot // GROUP, spot % GROUP], send_a_sem, recv_a_sem),
            (send_b.at[unit], recv_b.at[spot], send_b_sem, recv_b_sem),
        )
        if own:
            return [
                pltpu.make_async_copy(source, place, arrived.at[spot])
                for source, place, _, arrived in pairs
            ]
        return [
            pltpu.make_async_remote_copy(
                src_ref=source,
                dst_ref=place,
                send_sem=sent.at[unit],
                recv_sem=arrived.at[spot],
                device_id={"expert": expert},
                device_id_type=MESH,
            )
            for source, place, sent, arrived in pairs
        ]

    rows = GROUP * 2 * GROUP
    block = 512 if width % 512 == 0 else 256

    @pl.loop(0, chunks)
    def _(chunk):
        local_row = lax.broadcasted_iota(jnp.int32, (rows + 2 * GROUP, 1), 0)
        spare = local_row >= rows
        row_id = jnp.where(
            spare, full_rows + chunk * 2 * GROUP + local_row - rows, chunk * rows + local_row
        )
        is_x = jnp.where(spare, local_row % 2, local_row % (2 * GROUP) // GROUP) == 0
        x0 = row_id == row_x[:, :n_tok]
        x1 = row_id == row_x[:, n_tok:]
        g0 = row_id == row_g[:, :n_tok]
        g1 = row_id == row_g[:, n_tok:]
        pick = jnp.concatenate(
            [x0.astype(F32) + x1.astype(F32), g0.astype(F32) + g1.astype(F32)], axis=1
        ).astype(BF16)
        gate = jnp.where(g0, gate_ref[0:1, :], 0.0) + jnp.where(g1, gate_ref[1:2, :], 0.0)
        gate = jnp.sum(gate, axis=1, keepdims=True)
        scale = jnp.where(is_x, 1.0, gate)
        for lane in range(0, width, block):
            part = jnp.dot(pick, xg[:, lane : lane + block], preferred_element_type=F32) * scale
            send_a[pl.ds(chunk * GROUP, GROUP), :, lane : lane + block] = (
                part[:rows].astype(BF16).reshape(GROUP, 2 * GROUP, block)
            )
            row_scr[:, lane : lane + block] = part[rows:]
        for i in range(GROUP):
            send_b[chunk * GROUP + i] = row_scr[2 * i : 2 * i + 2, :].astype(BF16)

        @pl.loop(0, GROUP)
        def _(i):
            unit = chunk * GROUP + i
            own = target_of(unit)[0] == me

            @pl.when(own)
            def _():
                for copy in dispatch(unit, True):
                    copy.start()

            @pl.when(jnp.logical_not(own))
            def _():
                for copy in dispatch(unit, False):
                    copy.start()

    def weight_arrive(mat, h, of_dp, sem):
        part = (w_full, v_full)[mat].at[of_dp, h]
        pltpu.make_async_copy(part, part, sem).wait()

    for mat in range(2):
        for h in range(2):
            weight_arrive(mat, h, dp, wz_recv_sem.at[mat, h])
            for up in range(2):
                weight_pass(mat, h, dp, up).start()
    for h in range(2):
        weight_arrive(0, h, dp_down, wy_recv_sem.at[0, h, dp_down])
        weight_pass(0, h, dp_down, 1).start()
        weight_arrive(1, h, dp_up, wy_recv_sem.at[1, h, dp_up])
        weight_pass(1, h, dp_up, 0).start()
    for h in range(2):
        weight_arrive(0, h, dp_up, wy_recv_sem.at[0, h, dp_up])
        weight_arrive(1, h, dp_down, wy_recv_sem.at[1, h, dp_down])
        for mat in range(2):
            opposite = (dp + 2) % n_dp
            weight_arrive(mat, h, opposite, wy_recv_sem.at[mat, h, opposite])

    def give_back(unit):
        return [
            pltpu.make_async_remote_copy(
                src_ref=source.at[unit],
                dst_ref=home.at[host_chip],
                send_sem=sent.at[unit],
                recv_sem=arrived.at[host_chip],
                device_id={"section": other_section, "expert": source_of(unit)},
                device_id_type=MESH,
            )
            for source, home, sent, arrived in (
                (back_a, home_a, back_a_sem, home_a_sem),
                (back_b, home_b, back_b_sem, home_b_sem),
            )
        ]

    tall = 2 * GROUP * (GROUP + 1)
    short = GROUP * (GROUP + 1)

    @pl.loop(0, chunks)
    def _(chunk):
        @pl.loop(0, GROUP)
        def _(i):
            unit = chunk * GROUP + i
            a_ref = recv_a.at[chunk, i]
            pltpu.make_async_copy(a_ref, a_ref, recv_a_sem.at[unit]).wait()
            b_ref = recv_b.at[unit]
            pltpu.make_async_copy(b_ref, b_ref, recv_b_sem.at[unit]).wait()

        for i in range(GROUP):
            pair = recv_b[chunk * GROUP + i].astype(F32)
            row_scr[i : i + 1, :] = pair[0:1]
            row_scr[GROUP + i : GROUP + i + 1, :] = pair[1:2]
        recv_a[chunk, GROUP] = row_scr[...].astype(BF16)

        @pl.loop(0, n_dp)
        def _(y):
            def product(full, offset):
                total = None
                for h in range(2):
                    left = recv_a[chunk, :, :, h * half : (h + 1) * half].reshape(tall, half)
                    part = jnp.dot(left, full[y, h], preferred_element_type=F32)
                    part = part.reshape(GROUP + 1, 2 * GROUP, quarter)
                    part = part[:, offset : offset + GROUP, :].astype(BF16).astype(F32)
                    total = part if total is None else total + part
                return total

            pre = product(w_full, 0)
            hid = product(v_full, GROUP)
            act[y] = (hid * silu_slope(pre)).reshape(short, quarter).astype(BF16)

        lanes = 256 if half % 256 == 0 else half
        for h in range(2):
            for lane in range(0, half, lanes):
                total = None
                for y in range(n_dp):
                    part = lax.dot_general(
                        act[y],
                        w_full[y, h, lane : lane + lanes, :],
                        (((1,), (1,)), ((), ())),
                        preferred_element_type=F32,
                    )
                    total = part if total is None else total + part
                left = h * half + lane
                back_a[pl.ds(chunk * GROUP, GROUP), :, left : left + lanes] = (
                    total[: GROUP * GROUP].reshape(GROUP, GROUP, lanes).astype(BF16)
                )
                row_scr[:GROUP, left : left + lanes] = total[GROUP * GROUP :]
        for i in range(GROUP):
            back_b[chunk * GROUP + i] = jnp.concatenate(
                [row_scr[i : i + 1, :half], row_scr[i : i + 1, half:]], axis=0
            ).astype(BF16)

        @pl.loop(0, GROUP)
        def _(i):
            for copy in give_back(chunk * GROUP + i):
                copy.start()

    hand(0).wait_recv()
    hand(1).wait_recv()

    @pl.loop(0, chips)
    def _(chip):
        a_ref = home_a.at[chip]
        pltpu.make_async_copy(a_ref, a_ref, home_a_sem.at[chip]).wait()
        b_ref = home_b.at[chip]
        pltpu.make_async_copy(b_ref, b_ref, home_b_sem.at[chip]).wait()

    for chip in range(chips):
        pair = home_b[chip].astype(F32)
        home_scr[chip : chip + 1, :half] = pair[0:1]
        home_scr[chip : chip + 1, half:] = pair[1:2]
    for lane in range(0, width, block):
        span = slice(lane, lane + block)
        main = home_a[:, :, span].astype(F32).reshape(chips * GROUP, block).astype(BF16)
        total = jnp.dot(
            partner_combine[:, : chips * GROUP], main, preferred_element_type=F32
        ) + jnp.dot(
            partner_combine[:, chips * GROUP : chips * GROUP + chips],
            home_scr[:, span].astype(BF16),
            preferred_element_type=F32,
        )
        out_ref[:, span] = (partner_grad[:, span].astype(F32) + total).astype(BF16)

    hand(0).wait_send()
    hand(1).wait_send()
    for mat in range(2):
        for to_side in range(2):
            weight_send(mat, to_side).wait_send()
        for h in range(2):
            for up in range(2):
                weight_pass(mat, h, dp, up).wait_send()
    for h in range(2):
        weight_pass(0, h, dp_down, 1).wait_send()
        weight_pass(1, h, dp_up, 0).wait_send()

    @pl.loop(0, chips)
    def _(unit):
        @pl.when(target_of(unit)[0] != me)
        def _():
            for copy in dispatch(unit, False):
                copy.wait_send()

        for copy in give_back(unit):
            copy.wait_send()


def call(ring, n_dp, tokens, grads, ids, gates, w_in, w_out):
    n_tok, width = tokens.shape
    half = width // 2
    quarter = w_in.shape[1]
    chips = 2 * ring
    chunks = chips // GROUP
    slot_rows = -(-(chips * (GROUP + 1)) // 128) * 128
    dma = pltpu.SemaphoreType.DMA
    any_spec = pl.BlockSpec(memory_space=pl.ANY)
    vmem_spec = pl.BlockSpec(memory_space=pltpu.VMEM)
    return pl.pallas_call(
        functools.partial(kernel, ring, n_dp),
        out_shape=jax.ShapeDtypeStruct((n_tok, width), BF16),
        in_specs=[any_spec, any_spec, vmem_spec, vmem_spec, any_spec, any_spec],
        out_specs=vmem_spec,
        scratch_shapes=[
            pltpu.VMEM((2 * n_tok, width), BF16),
            pltpu.VMEM((n_tok, width), BF16),
            pltpu.VMEM((n_tok, slot_rows), BF16),
            pltpu.VMEM((n_tok, slot_rows), BF16),
            pltpu.VMEM((chips, 2 * GROUP, width), BF16),
            pltpu.VMEM((chips, 2, width), BF16),
            pltpu.VMEM((chunks, GROUP + 1, 2 * GROUP, width), BF16),
            pltpu.VMEM((chips, 2, width), BF16),
            pltpu.VMEM((chips, GROUP, width), BF16),
            pltpu.VMEM((chips, 2, half), BF16),
            pltpu.VMEM((chips, GROUP, width), BF16),
            pltpu.VMEM((chips, 2, half), BF16),
            pltpu.VMEM((n_dp, 2, half, quarter), BF16),
            pltpu.VMEM((n_dp, 2, half, quarter), BF16),
            pltpu.VMEM((n_dp, GROUP * (GROUP + 1), quarter), BF16),
            pltpu.VMEM((2 * GROUP, width), F32),
            pltpu.VMEM((chips, width), F32),
            dma((2,)),
            dma((chips,)),
            dma((chips,)),
            dma((chips,)),
            dma((chips,)),
            dma((chips,)),
            dma((chips,)),
            dma((chips,)),
            dma((chips,)),
            dma((2,)),
            dma((2,)),
            dma((2, 2)),
            dma((2, 2)),
            dma((2, 2, n_dp, 2)),
            dma((2, 2, n_dp)),
        ],
        compiler_params=pltpu.CompilerParams(
            collective_id=0, has_side_effects=True, vmem_limit_bytes=56 * 1024 * 1024
        ),
        name="routed_backward",
    )(tokens, grads, ids, gates, w_in, w_out)


def solution(mesh):
    ring = mesh.shape["expert"] // 4
    n_dp = mesh.shape["dp"]

    def body(tokens, grad_out, expert_ids, gate_values, w_in, w_out_t):
        handed = call(
            ring,
            n_dp,
            tokens[0],
            grad_out[0],
            expert_ids[0].T,
            gate_values[0].T,
            w_in[0, 0],
            w_out_t[0, 0],
        )
        return handed[None]

    return jax.shard_map(
        body,
        mesh=mesh,
        in_specs=(
            P("section", ("expert", "dp"), None),
            P("section", ("expert", "dp"), None),
            P("section", ("expert", "dp"), None),
            P("section", ("expert", "dp"), None),
            P("section", "expert", None, "dp"),
            P("section", "expert", None, "dp"),
        ),
        out_specs=P("section", ("expert", "dp"), None),
        check_vma=False,
    )
```

```python
import functools

import jax
import jax.numpy as jnp
from jax import lax
from jax.experimental import pallas as pl
from jax.experimental.pallas import tpu as pltpu
from jax.sharding import PartitionSpec as P

MESH = pl.DeviceIdType.MESH
F32 = jnp.float32
BF16 = jnp.bfloat16
GROUP = 8
REACH = 2


def silu_slope(pre):
    sig = 1.0 / (1.0 + jnp.exp(-pre))
    return sig * (1.0 + pre * (1.0 - sig))


def kernel(
    ring,
    n_dp,
    tok_ref,
    grad_ref,
    ids_ref,
    gate_ref,
    win_ref,
    wout_ref,
    out_ref,
    xg,
    partner_grad,
    combine,
    partner_combine,
    send_a,
    send_b,
    recv_a,
    recv_b,
    back_a,
    back_b,
    home_a,
    home_b,
    w_full,
    v_full,
    act,
    row_scr,
    home_scr,
    load_sem,
    send_a_sem,
    send_b_sem,
    recv_a_sem,
    recv_b_sem,
    back_a_sem,
    back_b_sem,
    home_a_sem,
    home_b_sem,
    hand_send_sem,
    hand_recv_sem,
    wz_send_sem,
    wz_recv_sem,
    wy_send_sem,
    wy_recv_sem,
):
    n_tok, width = tok_ref.shape
    half = width // 2
    quarter = win_ref.shape[1]
    chips = 2 * ring
    far = ring // 2
    chunks = chips // GROUP
    section = lax.axis_index("section")
    me = lax.axis_index("expert")
    dp = lax.axis_index("dp")
    core = me % 2
    my_xh = me // 2 % 2
    my_z = me // 4
    other_section = 1 - section
    dp_up, dp_down = (dp + 1) % n_dp, (dp + n_dp - 1) % n_dp

    side = 1 - 2 * core
    host_z = (my_z + REACH * side + ring) % ring
    host_chip = 2 * host_z + my_xh

    def index_of(z, xh, which_core):
        return 4 * ((z + 2 * ring) % ring) + 2 * xh + which_core

    def steps_of(place):
        place = (place + ring - 1) % ring
        odd = place % 2
        hop = far - (place + odd) // 2
        return jnp.where((odd == 1) | (place == 0), hop, -hop)

    def target_of(unit):
        d = steps_of(unit // 2)
        to_side = jnp.where(
            d == far, core, jnp.where(d == 0, 1 - core, (d < 0).astype(jnp.int32))
        )
        expert = index_of(my_z + d - REACH * (1 - 2 * to_side), unit % 2, to_side)
        even = (d == far) | (d == 0)
        spot = jnp.where(
            even,
            jnp.where(d == 0, 2, 0) + my_xh,
            4 * (far - jnp.abs(d)) + 2 * core + my_xh,
        )
        return expert, spot

    def source_of(spot):
        step = spot // 4
        d = jnp.where(step == 0, jnp.where(spot < 2, far, 0), side * (far - step))
        their_core = jnp.where(
            step == 0, jnp.where(spot < 2, core, 1 - core), spot // 2 % 2
        )
        return index_of(host_z - d, spot % 2, their_core)

    barrier = pltpu.get_barrier_semaphore()

    def greet(**where):
        pl.semaphore_signal(barrier, inc=1, device_id=where, device_id_type=MESH)

    for where in (0, 1):
        greet(expert=index_of(host_z, my_xh, where))
    for where in (dp_up, dp_down):
        greet(dp=where)
    greet(section=other_section)

    @pl.loop(0, chips)
    def _(i):
        expert = source_of(i)

        @pl.when(expert != me)
        def _():
            greet(expert=expert)

        greet(section=other_section, expert=target_of(i)[0])

    load_tok = pltpu.make_async_copy(tok_ref, xg.at[pl.ds(0, n_tok)], load_sem.at[0])
    load_grad = pltpu.make_async_copy(grad_ref, xg.at[pl.ds(n_tok, n_tok)], load_sem.at[1])
    load_tok.start()
    load_grad.start()

    ids = jnp.concatenate([ids_ref[0:1, :], ids_ref[1:2, :]], axis=1)
    flat = 2 * n_tok
    hot = (lax.broadcasted_iota(jnp.int32, (chips, flat), 0) == ids).astype(F32)
    earlier = (
        lax.broadcasted_iota(jnp.int32, (flat, flat), 0)
        < lax.broadcasted_iota(jnp.int32, (flat, flat), 1)
    ).astype(F32)
    before = jnp.dot(hot.astype(BF16), earlier.astype(BF16), preferred_element_type=F32)
    rank = jnp.sum(hot * before, axis=0, keepdims=True).astype(jnp.int32)
    apart = (ids // 2 - my_z + ring) % ring
    hops = jnp.minimum(apart, ring - apart)
    place = (2 * (far - hops) - (apart < far).astype(jnp.int32) + 1) % ring
    unit = 2 * place + ids % 2
    extra = rank >= GROUP
    full_rows = chips * 2 * GROUP
    row_x = jnp.where(extra, full_rows + 2 * unit, unit * 2 * GROUP + rank)
    row_g = jnp.where(extra, row_x + 1, row_x + GROUP)
    slot = jnp.where(extra, chips * GROUP + ids, ids * GROUP + rank)

    slot_rows = combine.shape[1]
    slot_iota = lax.broadcasted_iota(jnp.int32, (slot_rows, n_tok), 0)
    picks = (slot_iota == slot[:, :n_tok]).astype(F32) + (slot_iota == slot[:, n_tok:]).astype(F32)
    combine[...] = jnp.transpose(picks).astype(BF16)

    pl.semaphore_wait(barrier, 2 * chips - 1 + 5)

    def weight_send(mat, to_side):
        return pltpu.make_async_remote_copy(
            src_ref=(win_ref, wout_ref)[mat],
            dst_ref=(w_full, v_full)[mat].at[dp, core],
            send_sem=wz_send_sem.at[mat, to_side],
            recv_sem=wz_recv_sem.at[mat, core],
            device_id={
                "expert": index_of(my_z - REACH * (1 - 2 * to_side), my_xh, to_side)
            },
            device_id_type=MESH,
        )

    def weight_pass(mat, h, of_dp, up):
        part = (w_full, v_full)[mat].at[of_dp, h]
        return pltpu.make_async_remote_copy(
            src_ref=part,
            dst_ref=part,
            send_sem=wy_send_sem.at[mat, h, of_dp, up],
            recv_sem=wy_recv_sem.at[mat, h, of_dp],
            device_id={"dp": dp_up if up else dp_down},
            device_id_type=MESH,
        )

    for mat in range(2):
        for to_side in range(2):
            weight_send(mat, to_side).start()

    def hand(which):
        return pltpu.make_async_remote_copy(
            src_ref=(grad_ref, combine)[which],
            dst_ref=(partner_grad, partner_combine)[which],
            send_sem=hand_send_sem.at[which],
            recv_sem=hand_recv_sem.at[which],
            device_id={"section": other_section},
            device_id_type=MESH,
        )

    hand(0).start()
    hand(1).start()

    load_tok.wait()
    load_grad.wait()

    def dispatch(unit, own):
        expert, spot = target_of(unit)
        pairs = (
            (send_a.at[unit], recv_a.at[spot // GROUP, spot % GROUP], send_a_sem, recv_a_sem),
            (send_b.at[unit], recv_b.at[spot], send_b_sem, recv_b_sem),
        )
        if own:
            return [
                pltpu.make_async_copy(source, place, arrived.at[spot])
                for source, place, _, arrived in pairs
            ]
        return [
            pltpu.make_async_remote_copy(
                src_ref=source,
                dst_ref=place,
                send_sem=sent.at[unit],
                recv_sem=arrived.at[spot],
                device_id={"expert": expert},
                device_id_type=MESH,
            )
            for source, place, sent, arrived in pairs
        ]

    rows = GROUP * 2 * GROUP
    block = 512 if width % 512 == 0 else 256

    def weight_arrive(mat, h, of_dp, sem):
        part = (w_full, v_full)[mat].at[of_dp, h]
        pltpu.make_async_copy(part, part, sem).wait()

    for mat in range(2):
        for h in range(2):
            weight_arrive(mat, h, dp, wz_recv_sem.at[mat, h])
            for up in range(2):
                weight_pass(mat, h, dp, up).start()

    def send_rows(chunk):
        local_row = lax.broadcasted_iota(jnp.int32, (rows + 2 * GROUP, 1), 0)
        spare = local_row >= rows
        row_id = jnp.where(
            spare, full_rows + chunk * 2 * GROUP + local_row - rows, chunk * rows + local_row
        )
        is_x = jnp.where(spare, local_row % 2, local_row % (2 * GROUP) // GROUP) == 0
        x0 = row_id == row_x[:, :n_tok]
        x1 = row_id == row_x[:, n_tok:]
        g0 = row_id == row_g[:, :n_tok]
        g1 = row_id == row_g[:, n_tok:]
        pick = jnp.concatenate(
            [x0.astype(F32) + x1.astype(F32), g0.astype(F32) + g1.astype(F32)], axis=1
        ).astype(BF16)
        gate = jnp.where(g0, gate_ref[0:1, :], 0.0) + jnp.where(g1, gate_ref[1:2, :], 0.0)
        gate = jnp.sum(gate, axis=1, keepdims=True)
        scale = jnp.where(is_x, 1.0, gate)
        for lane in range(0, width, block):
            part = jnp.dot(pick, xg[:, lane : lane + block], preferred_element_type=F32) * scale
            send_a[pl.ds(chunk * GROUP, GROUP), :, lane : lane + block] = (
                part[:rows].astype(BF16).reshape(GROUP, 2 * GROUP, block)
            )
            row_scr[:, lane : lane + block] = part[rows:]
        for i in range(GROUP):
            send_b[chunk * GROUP + i] = row_scr[2 * i : 2 * i + 2, :].astype(BF16)

        @pl.loop(0, GROUP)
        def _(i):
            unit = chunk * GROUP + i
            own = target_of(unit)[0] == me

            @pl.when(own)
            def _():
                for copy in dispatch(unit, True):
                    copy.start()

            @pl.when(jnp.logical_not(own))
            def _():
                for copy in dispatch(unit, False):
                    copy.start()

    send_rows(0)
    for h in range(2):
        weight_arrive(0, h, dp_down, wy_recv_sem.at[0, h, dp_down])
        weight_pass(0, h, dp_down, 1).start()
        weight_arrive(1, h, dp_up, wy_recv_sem.at[1, h, dp_up])
        weight_pass(1, h, dp_up, 0).start()

    @pl.loop(1, chunks)
    def _(chunk):
        send_rows(chunk)

    for h in range(2):
        weight_arrive(0, h, dp_up, wy_recv_sem.at[0, h, dp_up])
        weight_arrive(1, h, dp_down, wy_recv_sem.at[1, h, dp_down])
        for mat in range(2):
            opposite = (dp + 2) % n_dp
            weight_arrive(mat, h, opposite, wy_recv_sem.at[mat, h, opposite])

    def give_back(unit):
        return [
            pltpu.make_async_remote_copy(
                src_ref=source.at[unit],
                dst_ref=home.at[host_chip],
                send_sem=sent.at[unit],
                recv_sem=arrived.at[host_chip],
                device_id={"section": other_section, "expert": source_of(unit)},
                device_id_type=MESH,
            )
            for source, home, sent, arrived in (
                (back_a, home_a, back_a_sem, home_a_sem),
                (back_b, home_b, back_b_sem, home_b_sem),
            )
        ]

    tall = 2 * GROUP * (GROUP + 1)
    short = GROUP * (GROUP + 1)

    @pl.loop(0, chunks)
    def _(chunk):
        @pl.loop(0, GROUP)
        def _(i):
            unit = chunk * GROUP + i
            a_ref = recv_a.at[chunk, i]
            pltpu.make_async_copy(a_ref, a_ref, recv_a_sem.at[unit]).wait()
            b_ref = recv_b.at[unit]
            pltpu.make_async_copy(b_ref, b_ref, recv_b_sem.at[unit]).wait()

        for i in range(GROUP):
            pair = recv_b[chunk * GROUP + i].astype(F32)
            row_scr[i : i + 1, :] = pair[0:1]
            row_scr[GROUP + i : GROUP + i + 1, :] = pair[1:2]
        recv_a[chunk, GROUP] = row_scr[...].astype(BF16)

        @pl.loop(0, n_dp)
        def _(y):
            def product(full, offset):
                total = None
                for h in range(2):
                    left = recv_a[chunk, :, :, h * half : (h + 1) * half].reshape(tall, half)
                    part = jnp.dot(left, full[y, h], preferred_element_type=F32)
                    part = part.reshape(GROUP + 1, 2 * GROUP, quarter)
                    part = part[:, offset : offset + GROUP, :].astype(BF16).astype(F32)
                    total = part if total is None else total + part
                return total

            pre = product(w_full, 0)
            hid = product(v_full, GROUP)
            act[y] = (hid * silu_slope(pre)).reshape(short, quarter).astype(BF16)

        lanes = 256 if half % 256 == 0 else half
        for h in range(2):
            for lane in range(0, half, lanes):
                total = None
                for y in range(n_dp):
                    part = lax.dot_general(
                        act[y],
                        w_full[y, h, lane : lane + lanes, :],
                        (((1,), (1,)), ((), ())),
                        preferred_element_type=F32,
                    )
                    total = part if total is None else total + part
                left = h * half + lane
                back_a[pl.ds(chunk * GROUP, GROUP), :, left : left + lanes] = (
                    total[: GROUP * GROUP].reshape(GROUP, GROUP, lanes).astype(BF16)
                )
                row_scr[:GROUP, left : left + lanes] = total[GROUP * GROUP :]
        for i in range(GROUP):
            back_b[chunk * GROUP + i] = jnp.concatenate(
                [row_scr[i : i + 1, :half], row_scr[i : i + 1, half:]], axis=0
            ).astype(BF16)

        @pl.loop(0, GROUP)
        def _(i):
            for copy in give_back(chunk * GROUP + i):
                copy.start()

    hand(0).wait_recv()
    hand(1).wait_recv()

    @pl.loop(0, chips)
    def _(chip):
        a_ref = home_a.at[chip]
        pltpu.make_async_copy(a_ref, a_ref, home_a_sem.at[chip]).wait()
        b_ref = home_b.at[chip]
        pltpu.make_async_copy(b_ref, b_ref, home_b_sem.at[chip]).wait()

    for chip in range(chips):
        pair = home_b[chip].astype(F32)
        home_scr[chip : chip + 1, :half] = pair[0:1]
        home_scr[chip : chip + 1, half:] = pair[1:2]
    for lane in range(0, width, block):
        span = slice(lane, lane + block)
        main = home_a[:, :, span].astype(F32).reshape(chips * GROUP, block).astype(BF16)
        total = jnp.dot(
            partner_combine[:, : chips * GROUP], main, preferred_element_type=F32
        ) + jnp.dot(
            partner_combine[:, chips * GROUP : chips * GROUP + chips],
            home_scr[:, span].astype(BF16),
            preferred_element_type=F32,
        )
        out_ref[:, span] = (partner_grad[:, span].astype(F32) + total).astype(BF16)

    hand(0).wait_send()
    hand(1).wait_send()
    for mat in range(2):
        for to_side in range(2):
            weight_send(mat, to_side).wait_send()
        for h in range(2):
            for up in range(2):
                weight_pass(mat, h, dp, up).wait_send()
    for h in range(2):
        weight_pass(0, h, dp_down, 1).wait_send()
        weight_pass(1, h, dp_up, 0).wait_send()

    @pl.loop(0, chips)
    def _(unit):
        @pl.when(target_of(unit)[0] != me)
        def _():
            for copy in dispatch(unit, False):
                copy.wait_send()

        for copy in give_back(unit):
            copy.wait_send()


def call(ring, n_dp, tokens, grads, ids, gates, w_in, w_out):
    n_tok, width = tokens.shape
    half = width // 2
    quarter = w_in.shape[1]
    chips = 2 * ring
    chunks = chips // GROUP
    slot_rows = -(-(chips * (GROUP + 1)) // 128) * 128
    dma = pltpu.SemaphoreType.DMA
    any_spec = pl.BlockSpec(memory_space=pl.ANY)
    vmem_spec = pl.BlockSpec(memory_space=pltpu.VMEM)
    return pl.pallas_call(
        functools.partial(kernel, ring, n_dp),
        out_shape=jax.ShapeDtypeStruct((n_tok, width), BF16),
        in_specs=[any_spec, any_spec, vmem_spec, vmem_spec, any_spec, any_spec],
        out_specs=vmem_spec,
        scratch_shapes=[
            pltpu.VMEM((2 * n_tok, width), BF16),
            pltpu.VMEM((n_tok, width), BF16),
            pltpu.VMEM((n_tok, slot_rows), BF16),
            pltpu.VMEM((n_tok, slot_rows), BF16),
            pltpu.VMEM((chips, 2 * GROUP, width), BF16),
            pltpu.VMEM((chips, 2, width), BF16),
            pltpu.VMEM((chunks, GROUP + 1, 2 * GROUP, width), BF16),
            pltpu.VMEM((chips, 2, width), BF16),
            pltpu.VMEM((chips, GROUP, width), BF16),
            pltpu.VMEM((chips, 2, half), BF16),
            pltpu.VMEM((chips, GROUP, width), BF16),
            pltpu.VMEM((chips, 2, half), BF16),
            pltpu.VMEM((n_dp, 2, half, quarter), BF16),
            pltpu.VMEM((n_dp, 2, half, quarter), BF16),
            pltpu.VMEM((n_dp, GROUP * (GROUP + 1), quarter), BF16),
            pltpu.VMEM((2 * GROUP, width), F32),
            pltpu.VMEM((chips, width), F32),
            dma((2,)),
            dma((chips,)),
            dma((chips,)),
            dma((chips,)),
            dma((chips,)),
            dma((chips,)),
            dma((chips,)),
            dma((chips,)),
            dma((chips,)),
            dma((2,)),
            dma((2,)),
            dma((2, 2)),
            dma((2, 2)),
            dma((2, 2, n_dp, 2)),
            dma((2, 2, n_dp)),
        ],
        compiler_params=pltpu.CompilerParams(
            collective_id=0, has_side_effects=True, vmem_limit_bytes=56 * 1024 * 1024
        ),
        name="routed_backward",
    )(tokens, grads, ids, gates, w_in, w_out)


def solution(mesh):
    ring = mesh.shape["expert"] // 4
    n_dp = mesh.shape["dp"]

    def body(tokens, grad_out, expert_ids, gate_values, w_in, w_out_t):
        handed = call(
            ring,
            n_dp,
            tokens[0],
            grad_out[0],
            expert_ids[0].T,
            gate_values[0].T,
            w_in[0, 0],
            w_out_t[0, 0],
        )
        return handed[None]

    return jax.shard_map(
        body,
        mesh=mesh,
        in_specs=(
            P("section", ("expert", "dp"), None),
            P("section", ("expert", "dp"), None),
            P("section", ("expert", "dp"), None),
            P("section", ("expert", "dp"), None),
            P("section", "expert", None, "dp"),
            P("section", "expert", None, "dp"),
        ),
        out_specs=P("section", ("expert", "dp"), None),
        check_vma=False,
    )
```

```python
import functools

import jax
import jax.numpy as jnp
from jax import lax
from jax.experimental import pallas as pl
from jax.experimental.pallas import tpu as pltpu
from jax.sharding import PartitionSpec as P

MESH = pl.DeviceIdType.MESH
F32 = jnp.float32
BF16 = jnp.bfloat16
GROUP = 8
REACH = 2


def silu_slope(pre):
    sig = 1.0 / (1.0 + jnp.exp(-pre))
    return sig * (1.0 + pre * (1.0 - sig))


def kernel(
    ring,
    n_dp,
    tok_ref,
    grad_ref,
    ids_ref,
    gate_ref,
    win_ref,
    wout_ref,
    out_ref,
    xg,
    partner_grad,
    combine,
    partner_combine,
    send_a,
    send_b,
    recv_a,
    recv_b,
    back_a,
    back_b,
    home_a,
    home_b,
    w_full,
    v_full,
    act,
    row_scr,
    home_scr,
    load_sem,
    send_a_sem,
    send_b_sem,
    recv_a_sem,
    recv_b_sem,
    back_a_sem,
    back_b_sem,
    home_a_sem,
    home_b_sem,
    hand_send_sem,
    hand_recv_sem,
    wz_send_sem,
    wz_recv_sem,
    wy_send_sem,
    wy_recv_sem,
):
    n_tok, width = tok_ref.shape
    half = width // 2
    quarter = win_ref.shape[1]
    chips = 2 * ring
    far = ring // 2
    chunks = chips // GROUP
    section = lax.axis_index("section")
    me = lax.axis_index("expert")
    dp = lax.axis_index("dp")
    core = me % 2
    my_xh = me // 2 % 2
    my_z = me // 4
    other_section = 1 - section
    dp_up, dp_down = (dp + 1) % n_dp, (dp + n_dp - 1) % n_dp

    side = 1 - 2 * core
    host_z = (my_z + REACH * side + ring) % ring
    host_chip = 2 * host_z + my_xh

    def index_of(z, xh, which_core):
        return 4 * ((z + 2 * ring) % ring) + 2 * xh + which_core

    def steps_of(place):
        place = (place + ring - 1) % ring
        odd = place % 2
        hop = far - (place + odd) // 2
        return jnp.where((odd == 1) | (place == 0), hop, -hop)

    def target_of(unit):
        d = steps_of(unit // 2)
        to_side = jnp.where(
            d == far, core, jnp.where(d == 0, 1 - core, (d < 0).astype(jnp.int32))
        )
        expert = index_of(my_z + d - REACH * (1 - 2 * to_side), unit % 2, to_side)
        even = (d == far) | (d == 0)
        spot = jnp.where(
            even,
            jnp.where(d == 0, 2, 0) + my_xh,
            4 * (far - jnp.abs(d)) + 2 * core + my_xh,
        )
        return expert, spot

    def source_of(spot):
        step = spot // 4
        d = jnp.where(step == 0, jnp.where(spot < 2, far, 0), side * (far - step))
        their_core = jnp.where(
            step == 0, jnp.where(spot < 2, core, 1 - core), spot // 2 % 2
        )
        return index_of(host_z - d, spot % 2, their_core)

    barrier = pltpu.get_barrier_semaphore()

    def greet(**where):
        pl.semaphore_signal(barrier, inc=1, device_id=where, device_id_type=MESH)

    for where in (0, 1):
        greet(expert=index_of(host_z, my_xh, where))
    for where in (dp_up, dp_down):
        greet(dp=where)
    greet(section=other_section)

    @pl.loop(0, chips)
    def _(i):
        expert = source_of(i)

        @pl.when(expert != me)
        def _():
            greet(expert=expert)

        greet(section=other_section, expert=target_of(i)[0])

    load_tok = pltpu.make_async_copy(tok_ref, xg.at[pl.ds(0, n_tok)], load_sem.at[0])
    load_grad = pltpu.make_async_copy(grad_ref, xg.at[pl.ds(n_tok, n_tok)], load_sem.at[1])
    load_tok.start()
    load_grad.start()

    ids = jnp.concatenate([ids_ref[0:1, :], ids_ref[1:2, :]], axis=1)
    flat = 2 * n_tok
    hot = (lax.broadcasted_iota(jnp.int32, (chips, flat), 0) == ids).astype(F32)
    earlier = (
        lax.broadcasted_iota(jnp.int32, (flat, flat), 0)
        < lax.broadcasted_iota(jnp.int32, (flat, flat), 1)
    ).astype(F32)
    before = jnp.dot(hot.astype(BF16), earlier.astype(BF16), preferred_element_type=F32)
    rank = jnp.sum(hot * before, axis=0, keepdims=True).astype(jnp.int32)
    apart = (ids // 2 - my_z + ring) % ring
    hops = jnp.minimum(apart, ring - apart)
    place = (2 * (far - hops) - (apart < far).astype(jnp.int32) + 1) % ring
    unit = 2 * place + ids % 2
    extra = rank >= GROUP
    full_rows = chips * 2 * GROUP
    row_x = jnp.where(extra, full_rows + 2 * unit, unit * 2 * GROUP + rank)
    row_g = jnp.where(extra, row_x + 1, row_x + GROUP)
    slot = jnp.where(extra, chips * GROUP + ids, ids * GROUP + rank)

    slot_rows = combine.shape[1]
    slot_iota = lax.broadcasted_iota(jnp.int32, (slot_rows, n_tok), 0)
    picks = (slot_iota == slot[:, :n_tok]).astype(F32) + (slot_iota == slot[:, n_tok:]).astype(F32)
    combine[...] = jnp.transpose(picks).astype(BF16)

    pl.semaphore_wait(barrier, 2 * chips - 1 + 5)

    def weight_send(mat, to_side):
        return pltpu.make_async_remote_copy(
            src_ref=(win_ref, wout_ref)[mat],
            dst_ref=(w_full, v_full)[mat].at[dp, core],
            send_sem=wz_send_sem.at[mat, to_side],
            recv_sem=wz_recv_sem.at[mat, core],
            device_id={
                "expert": index_of(my_z - REACH * (1 - 2 * to_side), my_xh, to_side)
            },
            device_id_type=MESH,
        )

    def weight_pass(mat, h, of_dp, up):
        part = (w_full, v_full)[mat].at[of_dp, h]
        return pltpu.make_async_remote_copy(
            src_ref=part,
            dst_ref=part,
            send_sem=wy_send_sem.at[mat, h, of_dp, up],
            recv_sem=wy_recv_sem.at[mat, h, of_dp],
            device_id={"dp": dp_up if up else dp_down},
            device_id_type=MESH,
        )

    for mat in range(2):
        for to_side in range(2):
            weight_send(mat, to_side).start()

    def hand(which):
        return pltpu.make_async_remote_copy(
            src_ref=(grad_ref, combine)[which],
            dst_ref=(partner_grad, partner_combine)[which],
            send_sem=hand_send_sem.at[which],
            recv_sem=hand_recv_sem.at[which],
            device_id={"section": other_section},
            device_id_type=MESH,
        )

    hand(0).start()
    hand(1).start()

    load_tok.wait()
    load_grad.wait()

    def dispatch(unit, own):
        expert, spot = target_of(unit)
        pairs = (
            (send_a.at[unit], recv_a.at[spot // GROUP, spot % GROUP], send_a_sem, recv_a_sem),
            (send_b.at[unit], recv_b.at[spot], send_b_sem, recv_b_sem),
        )
        if own:
            return [
                pltpu.make_async_copy(source, place, arrived.at[spot])
                for source, place, _, arrived in pairs
            ]
        return [
            pltpu.make_async_remote_copy(
                src_ref=source,
                dst_ref=place,
                send_sem=sent.at[unit],
                recv_sem=arrived.at[spot],
                device_id={"expert": expert},
                device_id_type=MESH,
            )
            for source, place, sent, arrived in pairs
        ]

    rows = GROUP * 2 * GROUP
    block = 512 if width % 512 == 0 else 256

    def weight_arrive(mat, h, of_dp, sem):
        part = (w_full, v_full)[mat].at[of_dp, h]
        pltpu.make_async_copy(part, part, sem).wait()

    for mat in range(2):
        for h in range(2):
            weight_arrive(mat, h, dp, wz_recv_sem.at[mat, h])
            for up in range(2):
                weight_pass(mat, h, dp, up).start()

    def send_rows(chunk):
        local_row = lax.broadcasted_iota(jnp.int32, (rows + 2 * GROUP, 1), 0)
        spare = local_row >= rows
        row_id = jnp.where(
            spare, full_rows + chunk * 2 * GROUP + local_row - rows, chunk * rows + local_row
        )
        is_x = jnp.where(spare, local_row % 2, local_row % (2 * GROUP) // GROUP) == 0
        x0 = row_id == row_x[:, :n_tok]
        x1 = row_id == row_x[:, n_tok:]
        g0 = row_id == row_g[:, :n_tok]
        g1 = row_id == row_g[:, n_tok:]
        pick = jnp.concatenate(
            [x0.astype(F32) + x1.astype(F32), g0.astype(F32) + g1.astype(F32)], axis=1
        ).astype(BF16)
        gate = jnp.where(g0, gate_ref[0:1, :], 0.0) + jnp.where(g1, gate_ref[1:2, :], 0.0)
        gate = jnp.sum(gate, axis=1, keepdims=True)
        scale = jnp.where(is_x, 1.0, gate)
        for lane in range(0, width, block):
            part = jnp.dot(pick, xg[:, lane : lane + block], preferred_element_type=F32) * scale
            send_a[pl.ds(chunk * GROUP, GROUP), :, lane : lane + block] = (
                part[:rows].astype(BF16).reshape(GROUP, 2 * GROUP, block)
            )
            row_scr[:, lane : lane + block] = part[rows:]
        for i in range(GROUP):
            send_b[chunk * GROUP + i] = row_scr[2 * i : 2 * i + 2, :].astype(BF16)

        @pl.loop(0, GROUP)
        def _(i):
            unit = chunk * GROUP + i
            own = target_of(unit)[0] == me

            @pl.when(own)
            def _():
                for copy in dispatch(unit, True):
                    copy.start()

            @pl.when(jnp.logical_not(own))
            def _():
                for copy in dispatch(unit, False):
                    copy.start()

    send_rows(0)
    for h in range(2):
        weight_arrive(0, h, dp_down, wy_recv_sem.at[0, h, dp_down])
        weight_pass(0, h, dp_down, 1).start()
        weight_arrive(1, h, dp_up, wy_recv_sem.at[1, h, dp_up])
        weight_pass(1, h, dp_up, 0).start()
    send_rows(1)

    @pl.loop(0, GROUP)
    def _(unit):
        @pl.when(target_of(unit)[0] != me)
        def _():
            for copy in dispatch(unit, False):
                copy.wait_send()

    @pl.loop(2, chunks)
    def _(chunk):
        send_rows(chunk)

    for h in range(2):
        weight_arrive(0, h, dp_up, wy_recv_sem.at[0, h, dp_up])
        weight_arrive(1, h, dp_down, wy_recv_sem.at[1, h, dp_down])
        for mat in range(2):
            opposite = (dp + 2) % n_dp
            weight_arrive(mat, h, opposite, wy_recv_sem.at[mat, h, opposite])

    def give_back(unit):
        return [
            pltpu.make_async_remote_copy(
                src_ref=source.at[unit],
                dst_ref=home.at[host_chip],
                send_sem=sent.at[unit],
                recv_sem=arrived.at[host_chip],
                device_id={"section": other_section, "expert": source_of(unit)},
                device_id_type=MESH,
            )
            for source, home, sent, arrived in (
                (back_a, home_a, back_a_sem, home_a_sem),
                (back_b, home_b, back_b_sem, home_b_sem),
            )
        ]

    tall = 2 * GROUP * (GROUP + 1)
    short = GROUP * (GROUP + 1)

    @pl.loop(0, chunks)
    def _(chunk):
        @pl.loop(0, GROUP)
        def _(i):
            unit = chunk * GROUP + i
            a_ref = recv_a.at[chunk, i]
            pltpu.make_async_copy(a_ref, a_ref, recv_a_sem.at[unit]).wait()
            b_ref = recv_b.at[unit]
            pltpu.make_async_copy(b_ref, b_ref, recv_b_sem.at[unit]).wait()

        for i in range(GROUP):
            pair = recv_b[chunk * GROUP + i].astype(F32)
            row_scr[i : i + 1, :] = pair[0:1]
            row_scr[GROUP + i : GROUP + i + 1, :] = pair[1:2]
        recv_a[chunk, GROUP] = row_scr[...].astype(BF16)

        @pl.loop(0, n_dp)
        def _(y):
            def product(full, offset):
                total = None
                for h in range(2):
                    left = recv_a[chunk, :, :, h * half : (h + 1) * half].reshape(tall, half)
                    part = jnp.dot(left, full[y, h], preferred_element_type=F32)
                    part = part.reshape(GROUP + 1, 2 * GROUP, quarter)
                    part = part[:, offset : offset + GROUP, :].astype(BF16).astype(F32)
                    total = part if total is None else total + part
                return total

            pre = product(w_full, 0)
            hid = product(v_full, GROUP)
            act[y] = (hid * silu_slope(pre)).reshape(short, quarter).astype(BF16)

        lanes = 256 if half % 256 == 0 else half
        for h in range(2):
            for lane in range(0, half, lanes):
                total = None
                for y in range(n_dp):
                    part = lax.dot_general(
                        act[y],
                        w_full[y, h, lane : lane + lanes, :],
                        (((1,), (1,)), ((), ())),
                        preferred_element_type=F32,
                    )
                    total = part if total is None else total + part
                left = h * half + lane
                back_a[pl.ds(chunk * GROUP, GROUP), :, left : left + lanes] = (
                    total[: GROUP * GROUP].reshape(GROUP, GROUP, lanes).astype(BF16)
                )
                row_scr[:GROUP, left : left + lanes] = total[GROUP * GROUP :]
        for i in range(GROUP):
            back_b[chunk * GROUP + i] = jnp.concatenate(
                [row_scr[i : i + 1, :half], row_scr[i : i + 1, half:]], axis=0
            ).astype(BF16)

        @pl.loop(0, GROUP)
        def _(i):
            for copy in give_back(chunk * GROUP + i):
                copy.start()

    hand(0).wait_recv()
    hand(1).wait_recv()

    @pl.loop(0, chips)
    def _(chip):
        a_ref = home_a.at[chip]
        pltpu.make_async_copy(a_ref, a_ref, home_a_sem.at[chip]).wait()
        b_ref = home_b.at[chip]
        pltpu.make_async_copy(b_ref, b_ref, home_b_sem.at[chip]).wait()
        pair = home_b[chip].astype(F32)
        home_scr[pl.ds(chip, 1), :half] = pair[0:1]
        home_scr[pl.ds(chip, 1), half:] = pair[1:2]

    for lane in range(0, width, block):
        span = slice(lane, lane + block)
        main = home_a[:, :, span].astype(F32).reshape(chips * GROUP, block).astype(BF16)
        total = jnp.dot(
            partner_combine[:, : chips * GROUP], main, preferred_element_type=F32
        ) + jnp.dot(
            partner_combine[:, chips * GROUP : chips * GROUP + chips],
            home_scr[:, span].astype(BF16),
            preferred_element_type=F32,
        )
        out_ref[:, span] = (partner_grad[:, span].astype(F32) + total).astype(BF16)

    hand(0).wait_send()
    hand(1).wait_send()
    for mat in range(2):
        for to_side in range(2):
            weight_send(mat, to_side).wait_send()
        for h in range(2):
            for up in range(2):
                weight_pass(mat, h, dp, up).wait_send()
    for h in range(2):
        weight_pass(0, h, dp_down, 1).wait_send()
        weight_pass(1, h, dp_up, 0).wait_send()

    @pl.loop(0, chips)
    def _(unit):
        @pl.when((unit >= GROUP) & (target_of(unit)[0] != me))
        def _():
            for copy in dispatch(unit, False):
                copy.wait_send()

        for copy in give_back(unit):
            copy.wait_send()


def call(ring, n_dp, tokens, grads, ids, gates, w_in, w_out):
    n_tok, width = tokens.shape
    half = width // 2
    quarter = w_in.shape[1]
    chips = 2 * ring
    chunks = chips // GROUP
    slot_rows = -(-(chips * (GROUP + 1)) // 128) * 128
    dma = pltpu.SemaphoreType.DMA
    any_spec = pl.BlockSpec(memory_space=pl.ANY)
    vmem_spec = pl.BlockSpec(memory_space=pltpu.VMEM)
    return pl.pallas_call(
        functools.partial(kernel, ring, n_dp),
        out_shape=jax.ShapeDtypeStruct((n_tok, width), BF16),
        in_specs=[any_spec, any_spec, vmem_spec, vmem_spec, any_spec, any_spec],
        out_specs=vmem_spec,
        scratch_shapes=[
            pltpu.VMEM((2 * n_tok, width), BF16),
            pltpu.VMEM((n_tok, width), BF16),
            pltpu.VMEM((n_tok, slot_rows), BF16),
            pltpu.VMEM((n_tok, slot_rows), BF16),
            pltpu.VMEM((chips, 2 * GROUP, width), BF16),
            pltpu.VMEM((chips, 2, width), BF16),
            pltpu.VMEM((chunks, GROUP + 1, 2 * GROUP, width), BF16),
            pltpu.VMEM((chips, 2, width), BF16),
            pltpu.VMEM((chips, GROUP, width), BF16),
            pltpu.VMEM((chips, 2, half), BF16),
            pltpu.VMEM((chips, GROUP, width), BF16),
            pltpu.VMEM((chips, 2, half), BF16),
            pltpu.VMEM((n_dp, 2, half, quarter), BF16),
            pltpu.VMEM((n_dp, 2, half, quarter), BF16),
            pltpu.VMEM((n_dp, GROUP * (GROUP + 1), quarter), BF16),
            pltpu.VMEM((2 * GROUP, width), F32),
            pltpu.VMEM((chips, width), F32),
            dma((2,)),
            dma((chips,)),
            dma((chips,)),
            dma((chips,)),
            dma((chips,)),
            dma((chips,)),
            dma((chips,)),
            dma((chips,)),
            dma((chips,)),
            dma((2,)),
            dma((2,)),
            dma((2, 2)),
            dma((2, 2)),
            dma((2, 2, n_dp, 2)),
            dma((2, 2, n_dp)),
        ],
        compiler_params=pltpu.CompilerParams(
            collective_id=0, has_side_effects=True, vmem_limit_bytes=56 * 1024 * 1024
        ),
        name="routed_backward",
    )(tokens, grads, ids, gates, w_in, w_out)


def solution(mesh):
    ring = mesh.shape["expert"] // 4
    n_dp = mesh.shape["dp"]

    def body(tokens, grad_out, expert_ids, gate_values, w_in, w_out_t):
        handed = call(
            ring,
            n_dp,
            tokens[0],
            grad_out[0],
            expert_ids[0].T,
            gate_values[0].T,
            w_in[0, 0],
            w_out_t[0, 0],
        )
        return handed[None]

    return jax.shard_map(
        body,
        mesh=mesh,
        in_specs=(
            P("section", ("expert", "dp"), None),
            P("section", ("expert", "dp"), None),
            P("section", ("expert", "dp"), None),
            P("section", ("expert", "dp"), None),
            P("section", "expert", None, "dp"),
            P("section", "expert", None, "dp"),
        ),
        out_specs=P("section", ("expert", "dp"), None),
        check_vma=False,
    )
```
